32 devices in a mesh: region: 2 (over x), shard: 16 (over z, y, core).
Axes of the slice: x: 2, y: 2, z: 4, core: 2. Of those that a mesh axis runs over, the one named last changes fastest.
Arguments:
- queries: bfloat16 [48, 1024], replicated, may hold values from -6 to 6
- database: bfloat16 [16384, 1024], P(('region', 'shard')), may hold values from -6 to 6
- neighbour_ids: int32 [48, 10], replicated, may hold values from 0 to 16383
- tile_weights: bfloat16 [64, 13, 4, 256], P(('region', 'shard')), may hold values from 0.0019989014 to 0.059814453
- tile_columns: int32 [64, 13, 4, 256], P(('region', 'shard')), may hold values from 0 to 255
- tile_owner: int32 [64, 13], P(('region', 'shard')), may hold values from 0 to 15, all different within a row; in each aligned block of 2 rows (0 to 1, 2 to 3, ...) at most 2 rows name the same one
- tile_block: int32 [64, 13], P(('region', 'shard')), may hold values from 0 to 1
Outputs:
- diffused: float32 [48, 16384], P(None, ('region', 'shard'))
The draws below stay inside these ranges and needn't reach their ends.
Inputs may be any that keep to these rules, and one draw needn't show every extreme that they name: `tile_owner`: each row names 13 different owners; among the rows of one device's blocks no owner is named more than 2 times, and that many in some devices.
All inputs are finite; a program needn't handle non-finite values.
Results may differ from the reference program's by a relative error of at most 0.005.
Values may be sent and summed in bfloat16 or wider, within the bound.
A program may use at most 64 MiB of HBM per device.

```python
import math
import jax
import jax.numpy as jnp
import numpy as np
from jax import lax

D = 1024
NQ = 48
NEIGH = 10
BLK = 256
EDGES = 4
BLK_DEV = 2
NBR = 13
CAP = 2
SWEEPS = 2
NBLOCKS = 64
NROWS = 16384
N_SHARD = 16


def with_ends(array, stream_key, low, largest):
    longest = array.shape.index(max(array.shape))
    spots = []
    for shift in (0, 1):
        where = [jax.random.randint(jax.random.fold_in(stream_key, axis), (), 0, length) for axis, length in enumerate(array.shape)]
        where[longest] = (where[longest] + shift) % array.shape[longest]
        spots.append(tuple(where))
    return array.at[spots[0]].set(low).at[spots[1]].set(largest)


def block_levels(own_key, shape, cuts, least, largest):
    loudness, own = 1.0, jax.random.fold_in(own_key, 6)
    for axis_at, blocks in cuts:
        heights = jnp.exp(jax.random.uniform(jax.random.fold_in(own, axis_at), (blocks,), jnp.float32, least / len(cuts), largest / len(cuts)))
        loudness = loudness * jnp.repeat(heights, shape[axis_at] // blocks).reshape([-1 if axis == axis_at else 1 for axis in range(len(shape))])
    return loudness


def assign_block(key, own, number, rows, number_of, top, limit, slope):
    sequence = jax.random.permutation(key, number_of)
    packed, common = load_shares(number_of, rows * top, limit, slope, True), load_shares(number_of, rows * top, limit, slope, False)
    places = jnp.arange(number_of)

    def named(tallies, turn):
        used = int((tallies > 0).sum())
        fixed = max(1, used // 4)
        moved = fixed + (places - fixed + turn * (used - fixed)) % max(1, number_of - fixed)
        return jnp.zeros((number_of,), jnp.int32).at[sequence[jnp.where(places < fixed, places, moved)]].set(jnp.asarray(tallies, jnp.int32))

    tallies = jnp.where(number % 4 == 0, named(packed, number // 4), named(common, number - number // 4 - 1))
    mixed = jax.random.permutation(jax.random.fold_in(own, 3), number_of)
    source_of, sink = mixed[0:number_of // 2 * 2:2], mixed[1:number_of // 2 * 2:2]
    slack = jnp.minimum(tallies[source_of] - 1, limit - tallies[sink]) // 2
    slack = jnp.where((source_of == sequence[0]) | (sink == sequence[0]) | (tallies[sink] == 0), 0, jnp.maximum(slack, 0))
    moved = jax.random.randint(jax.random.fold_in(own, 4), (number_of // 2,), 0, 1 << 20) % (slack + 1)
    tallies = tallies.at[source_of].add(-moved).at[sink].add(moved)
    labels = jnp.searchsorted(jnp.cumsum(tallies), jnp.arange(rows * top), side="right").astype(jnp.int32)
    grid = labels.reshape(top, rows).T
    grid = grid[jax.random.permutation(jax.random.fold_in(own, 1), rows)]
    turn = jax.random.randint(jax.random.fold_in(own, 2), (rows, 1), 0, top)
    return jnp.take_along_axis(grid, (jnp.arange(top)[None, :] + turn) % top, axis=1)


def load_shares(count, total, reach, slope, full):
    loads = [(1 << 20) // math.isqrt(grade ** slope) + 1 for grade in range(1, count + 1)]
    largest = reach if full else min(reach, max(-(-total // count), total * loads[0] // sum(loads)))
    least = 1 if total - largest >= count - 1 else 0
    given, rest = [largest] + [least] * (count - 1), total - largest - least * (count - 1)
    while rest > 0:
        free = [i for i in range(1, count) if given[i] < largest] or [i for i in range(1, count) if given[i] < reach]
        pool, budget = sum([loads[i] for i in free]), rest
        for i in free:
            more = min(reach - given[i], max(1, budget * loads[i] // pool), rest)
            given[i] = given[i] + more
            rest = rest - more
    return np.array(given)


def bell_draw(own_key, extent, scale, most, split=(), kind=jnp.bfloat16):
    gain = block_levels(own_key, extent, split, -0.22, 0.18) if split else 1.0
    drawn = jax.random.normal(own_key, extent, jnp.float32) * scale * gain
    return jnp.minimum(jnp.maximum(drawn, -most), most).astype(kind)


def setup_inputs(seed: int = 0) -> dict:
    streams_of = jax.random.split(jax.random.key(seed), 8)
    queries = bell_draw(streams_of[0], (NQ, D), 1.0, 6.0)
    database = bell_draw(streams_of[1], (NROWS, D), 1.0, 6.0, ((0, 32),))
    neighbour_ids = with_ends(jax.random.randint(streams_of[2], (NQ, NEIGH), 0, NROWS), jax.random.fold_in(streams_of[2], 1), 0, NROWS - 1).astype(jnp.int32)
    tile_weights = jnp.clip(jnp.exp(math.log(0.059814453) - 3.3986496 * jax.random.uniform(streams_of[3], (NBLOCKS, NBR, EDGES, BLK), jnp.float32) ** block_levels(streams_of[3], (NBLOCKS, NBR, EDGES, BLK), ((0, 32),), -0.2, 0.2)), 0.0019989014, 0.059814453).astype(jnp.bfloat16)
    tile_columns = with_ends(jax.random.randint(streams_of[4], (NBLOCKS, NBR, EDGES, BLK), 0, BLK), jax.random.fold_in(streams_of[4], 1), 0, BLK - 1).astype(jnp.int32)
    tile_owner_keys = jax.random.split(jax.random.fold_in(streams_of[5], 1), NBLOCKS // BLK_DEV)
    tile_owner_turns = jax.random.permutation(jax.random.fold_in(streams_of[5], 3), NBLOCKS // BLK_DEV)
    tile_owner = jax.vmap(lambda own, number: assign_block(jax.random.fold_in(streams_of[5], 2), own, number, BLK_DEV, N_SHARD, NBR, CAP, 2))(tile_owner_keys, tile_owner_turns).reshape((NBLOCKS, NBR))
    tile_block = with_ends(jax.random.randint(streams_of[6], (NBLOCKS, NBR), 0, BLK_DEV), jax.random.fold_in(streams_of[6], 1), 0, BLK_DEV - 1).astype(jnp.int32)
    return {"queries": queries, "database": database, "neighbour_ids": neighbour_ids, "tile_weights": tile_weights, "tile_columns": tile_columns, "tile_owner": tile_owner, "tile_block": tile_block}


EPS = 1e-06
BETA = 0.8

def unit_rows(matrix):
    return matrix / jnp.sqrt(lax.optimization_barrier(jnp.sum(matrix * matrix, axis=1, keepdims=True)) + EPS)

def reference(queries, database, neighbour_ids, tile_weights, tile_columns, tile_owner, tile_block):
    unit_query = unit_rows(queries.astype(jnp.float32)).astype(jnp.bfloat16)
    fetched = jnp.take(database, neighbour_ids, axis=0).astype(jnp.float32)
    similar = jnp.einsum('qd,qkd->qk', unit_query.astype(jnp.float32), fetched)
    positive = jnp.maximum(similar, 0.0)
    weights = (positive * positive * positive / math.sqrt(D)).astype(jnp.bfloat16)
    expanded_sum = unit_query.astype(jnp.float32) + jnp.einsum('qk,qkd->qd', weights.astype(jnp.float32), fetched)
    expanded = unit_rows(expanded_sum).astype(jnp.bfloat16)
    products = lax.dot_general(expanded, database, (((1,), (1,)), ((), ())), preferred_element_type=jnp.float32)
    scores = jnp.maximum(products, 0.0).astype(jnp.bfloat16)
    region_span = N_SHARD * BLK_DEV
    block_index = jnp.arange(NBLOCKS, dtype=jnp.int32)[:, None]
    target = (block_index // region_span * region_span + tile_owner * BLK_DEV + tile_block).astype(jnp.int32)
    score_blocks = scores.reshape(NQ, NBLOCKS, BLK)

    def spread(current):
        flat = current.reshape(NQ, NROWS)

        def one_block(block_triple):
            weight_block, column_block, targets = block_triple
            index = (targets[:, None, None] * BLK + column_block).astype(jnp.int32)
            reached = jnp.take(flat, index, axis=1).astype(jnp.float32)
            return lax.optimization_barrier(jnp.sum(reached * weight_block.astype(jnp.float32)[None], axis=(1, 2)))
        result = lax.map(one_block, (tile_weights, tile_columns, target))
        return result.transpose(1, 0, 2)
    source = score_blocks.astype(jnp.float32)
    current = score_blocks
    for sweep_index in range(SWEEPS - 1):
        current = (source + BETA * spread(current)).astype(jnp.bfloat16)
    diffused = source + BETA * spread(current)
    return diffused.reshape(NQ, NROWS)
```

```python
import functools
import math

import jax
import jax.numpy as jnp
from jax import lax
from jax.experimental import pallas as pl
from jax.experimental.pallas import tpu as pltpu
from jax.sharding import PartitionSpec as P

EPS = 1e-06
BETA = 0.8
LANES = 128
F32 = jnp.float32
BF16 = jnp.bfloat16


def flip(index, mask):
    bit = 1
    while bit <= mask:
        if mask & bit:
            index = index + bit - 2 * bit * ((index // bit) % 2)
        bit *= 2
    return index


class Plan:
    def __init__(self, regions, shards, width):
        self.regions, self.shards = regions, shards
        self.slices = width // LANES
        self.inner = self.slices // regions
        self.outer = shards // self.inner
        assert self.inner * regions * LANES == width and self.outer * self.inner == shards
        assert self.inner == 1 or self.inner % 2 == 0
        if self.inner > 2:
            self.mid = self.inner // 2
        else:
            self.mid = 1 << (((shards // 2).bit_length() - 1) // 2)
        self.far = shards // (2 * self.mid)
        assert self.far * self.mid * 2 == shards


def kernel(
    plan,
    q_ref,
    db_hbm,
    ids_ref,
    w_ref,
    col_ref,
    owner_ref,
    block_ref,
    out_ref,
    db,
    uq,
    part,
    rs_buf,
    z_send,
    z_buf,
    full,
    tiles,
    scores_ref,
    all1,
    all2,
    load_sem,
    rs_sems,
    z_sems,
    ag_sems,
    far_sems,
    mid_sems,
    core_sems,
):
    rows_dev, width = db.shape
    blocks_dev, tile_count, edge_count, block_rows = w_ref.shape
    slices, inner, outer = plan.slices, plan.inner, plan.outer
    region, shard = lax.axis_index("region"), lax.axis_index("shard")
    group_at, group = shard % inner, shard // inner
    slot = region * inner + group_at

    def member(index):
        return (index // inner, group * inner + index % inner)

    def across(index):
        return (region, index * inner + group_at)

    load = pltpu.make_async_copy(db_hbm, db, load_sem)
    load.start()
    barrier = pltpu.get_barrier_semaphore()
    for d in range(1, slices):
        pl.semaphore_signal(
            barrier, inc=1, device_id=member(flip(slot, d)), device_id_type=pl.DeviceIdType.MESH
        )
    for d in range(1, outer):
        pl.semaphore_signal(
            barrier, inc=1, device_id=across(flip(group, d)), device_id_type=pl.DeviceIdType.MESH
        )

    def send(src, dst, sems, at, device):
        copy = pltpu.make_async_remote_copy(
            src_ref=src,
            dst_ref=dst,
            send_sem=sems.at[(0,) + at],
            recv_sem=sems.at[(1,) + at],
            device_id=device,
            device_id_type=pl.DeviceIdType.MESH,
        )
        copy.start()
        return copy

    row_of = lax.broadcasted_iota(jnp.int32, (block_rows, block_rows), 0).astype(F32).astype(BF16)

    def build(t, carry):
        b, j = t // tile_count, t % tile_count
        columns = col_ref[b, j].astype(F32).astype(BF16)
        weights = w_ref[b, j]
        acc = None
        for e in range(edge_count):
            hit = row_of == columns[e : e + 1, :]
            term = jnp.where(hit, weights[e : e + 1, :], jnp.zeros((), BF16))
            acc = term if acc is None else acc + term
        tiles[t] = acc
        return carry

    total_tiles = blocks_dev * tile_count
    cuts = [0, total_tiles * 3 // 10, total_tiles * 7 // 10, total_tiles]

    q = q_ref[...].astype(F32)
    unit = (q / jnp.sqrt(jnp.sum(q * q, axis=1, keepdims=True) + EPS)).astype(BF16)
    for p in range(slices):
        uq[p] = unit[:, p * LANES : (p + 1) * LANES].astype(F32)
    ids = ids_ref[...] - (region * plan.shards + shard) * rows_dev
    row_ids = lax.broadcasted_iota(jnp.int32, (ids.shape[0], rows_dev), 1)
    counts = jnp.zeros((ids.shape[0], rows_dev), F32)
    for k in range(ids.shape[1]):
        counts = counts + jnp.where(ids[:, k : k + 1] == row_ids, 1.0, 0.0)
    load.wait()
    data = db[...]
    similar = lax.dot_general(unit, data, (((1,), (1,)), ((), ())), preferred_element_type=F32)
    positive = jnp.maximum(similar, 0.0)
    weights = (positive * positive * positive / math.sqrt(width)).astype(BF16)
    chosen = (counts * weights.astype(F32)).astype(BF16)
    local = jnp.dot(chosen, data, preferred_element_type=F32)
    for p in range(slices):
        part[p] = local[:, p * LANES : (p + 1) * LANES].astype(BF16)

    pl.semaphore_wait(barrier, slices - 1 + outer - 1)

    copies = []
    for d in range(1, slices):
        peer = flip(slot, d)
        copies.append(send(part.at[peer], rs_buf.at[d], rs_sems, (d,), member(peer)))
    lax.fori_loop(cuts[0], cuts[1], build, 0)
    total = part[slot].astype(F32)
    for d in range(1, slices):
        copies[d - 1].wait_recv()
        total = total + rs_buf[d].astype(F32)
    z_send[...] = total.astype(BF16)
    pending = copies

    copies = []
    for d in range(1, outer):
        copies.append(send(z_send, z_buf.at[d], z_sems, (d,), across(flip(group, d))))
    lax.fori_loop(cuts[1], cuts[2], build, 0)
    total = total + uq[slot]
    for d in range(1, outer):
        copies[d - 1].wait_recv()
        total = total + z_buf[d].astype(F32)
    full[slot] = total.astype(BF16)
    pending = pending + copies

    copies = []
    for d in range(1, slices):
        copies.append(
            send(full.at[slot], full.at[slot], ag_sems, (d,), member(flip(slot, d)))
        )
    lax.fori_loop(cuts[2], cuts[3], build, 0)
    for copy in copies:
        copy.wait_recv()
    pending = pending + copies

    expanded = jnp.concatenate([full[p] for p in range(slices)], axis=1)
    wide = expanded.astype(F32)
    scale = 1.0 / jnp.sqrt(jnp.sum(wide * wide, axis=1, keepdims=True) + EPS)
    products = lax.dot_general(
        expanded, data, (((1,), (1,)), ((), ())), preferred_element_type=F32
    )
    scores = jnp.maximum(products * scale, 0.0).astype(BF16)

    mid, far = plan.mid, plan.far
    far_at, mid_at, core_at = shard // (2 * mid), (shard // 2) % mid, shard % 2

    def share(buf, which):
        def place(f, m, c):
            return (f * mid + m) * 2 + c

        done = []

        def push(f, m, sems, at, device):
            source = buf.at[place(f, m, core_at)]
            done.append(send(source, source, sems, (which,) + at, (region, device)))
            return done[-1]

        partner = place(far_at, mid_at, 1 - core_at)

        def to_mids(fd, f):
            return [
                push(f, mid_at, mid_sems, (md, fd), place(far_at, flip(mid_at, md), core_at))
                for md in range(1, mid)
            ]

        core_copies, mid_copies = [], []
        far_copies = [
            push(far_at, mid_at, far_sems, (fd,), place(flip(far_at, fd), mid_at, core_at))
            for fd in range(far - 1, 0, -1)
        ][::-1]
        mid_copies.append(to_mids(0, far_at))
        core_copies.append(push(far_at, mid_at, core_sems, (0, 0), partner))

        def mids_arrive(fd):
            for md in range(1, mid):
                mid_copies[fd][md - 1].wait_recv()
                core_copies.append(
                    push(flip(far_at, fd), flip(mid_at, md), core_sems, (md, fd), partner)
                )

        for fd in range(1, far):
            far_copies[fd - 1].wait_recv()
            mid_copies.append(to_mids(fd, flip(far_at, fd)))
            core_copies.append(push(flip(far_at, fd), mid_at, core_sems, (0, fd), partner))
            mids_arrive(fd - 1)
        mids_arrive(far - 1)
        for copy in core_copies:
            copy.wait_recv()
        return done

    def spread(buf):
        sums = []
        for b in range(blocks_dev):
            acc = None
            for j in range(tile_count):
                values = buf[owner_ref[b, j], block_ref[b, j]]
                term = jnp.dot(
                    values, tiles[b * tile_count + j], preferred_element_type=F32
                )
                acc = term if acc is None else acc + term
            sums.append(acc)
        return sums

    for b in range(blocks_dev):
        own = scores[:, b * block_rows : (b + 1) * block_rows]
        scores_ref[b] = own.astype(F32)
        all1[shard, b] = own
    pending = pending + share(all1, 0)
    sums = spread(all1)
    for b in range(blocks_dev):
        all2[shard, b] = (scores_ref[b] + BETA * sums[b]).astype(BF16)
    pending = pending + share(all2, 1)
    sums = spread(all2)
    for b in range(blocks_dev):
        out_ref[:, b * block_rows : (b + 1) * block_rows] = scores_ref[b] + BETA * sums[b]
    for copy in pending:
        copy.wait_send()


def per_device(
    plan, queries, database, neighbour_ids, tile_weights, tile_columns, tile_owner, tile_block
):
    query_count, width = queries.shape
    rows_dev = database.shape[0]
    blocks_dev, tile_count, edge_count, block_rows = tile_weights.shape
    vmem = pl.BlockSpec(memory_space=pltpu.VMEM)
    smem = pl.BlockSpec(memory_space=pltpu.SMEM)
    dma = pltpu.SemaphoreType.DMA
    state = (plan.shards, blocks_dev, query_count, block_rows)
    piece = (query_count, LANES)
    return pl.pallas_call(
        functools.partial(kernel, plan),
        out_shape=jax.ShapeDtypeStruct((query_count, rows_dev), F32),
        in_specs=[vmem, pl.BlockSpec(memory_space=pl.ANY), vmem, vmem, vmem, smem, smem],
        out_specs=vmem,
        scratch_shapes=[
            pltpu.VMEM((rows_dev, width), BF16),
            pltpu.VMEM((plan.slices,) + piece, F32),
            pltpu.VMEM((plan.slices,) + piece, BF16),
            pltpu.VMEM((plan.slices,) + piece, BF16),
            pltpu.VMEM(piece, BF16),
            pltpu.VMEM((plan.outer,) + piece, BF16),
            pltpu.VMEM((plan.slices,) + piece, BF16),
            pltpu.VMEM((blocks_dev * tile_count, block_rows, block_rows), BF16),
            pltpu.VMEM((blocks_dev, query_count, block_rows), F32),
            pltpu.VMEM(state, BF16),
            pltpu.VMEM(state, BF16),
            dma,
            dma((2, plan.slices)),
            dma((2, plan.outer)),
            dma((2, plan.slices)),
            dma((2, 2, plan.far)),
            dma((2, 2, plan.mid, plan.far)),
            dma((2, 2, plan.mid, plan.far)),
        ],
        compiler_params=pltpu.CompilerParams(collective_id=0, has_side_effects=True),
        name="expand_and_diffuse",
    )(queries, database, neighbour_ids, tile_weights, tile_columns, tile_owner, tile_block)


def solution(mesh):
    plan_of = functools.partial(Plan, mesh.shape["region"], mesh.shape["shard"])

    def body(queries, *rest):
        return per_device(plan_of(queries.shape[1]), queries, *rest)

    placed = (
        P(),
        P(("region", "shard"), None),
        P(),
        P(("region", "shard"), None, None, None),
        P(("region", "shard"), None, None, None),
        P(("region", "shard"), None),
        P(("region", "shard"), None),
    )
    return jax.shard_map(
        body,
        mesh=mesh,
        in_specs=placed,
        out_specs=P(None, ("region", "shard")),
        check_vma=False,
    )
```

```python
import functools
import math

import jax
import jax.numpy as jnp
from jax import lax
from jax.experimental import pallas as pl
from jax.experimental.pallas import tpu as pltpu
from jax.sharding import PartitionSpec as P

EPS = 1e-06
LAG = 2
BETA = 0.8
CUTS = (0, 5, 12, 17, 26)
LANES = 128
F32 = jnp.float32
BF16 = jnp.bfloat16


def flip(index, mask):
    bit = 1
    while bit <= mask:
        if mask & bit:
            index = index + bit - 2 * bit * ((index // bit) % 2)
        bit *= 2
    return index


class Plan:
    def __init__(self, regions, shards, width):
        self.regions, self.shards = regions, shards
        self.slices = width // LANES
        self.inner = self.slices // regions
        self.outer = shards // self.inner
        assert self.inner * regions * LANES == width and self.outer * self.inner == shards
        assert self.inner == 1 or self.inner % 2 == 0
        if self.inner > 2:
            self.mid = self.inner // 2
        else:
            self.mid = 1 << (((shards // 2).bit_length() - 1) // 2)
        self.far = shards // (2 * self.mid)
        assert self.far * self.mid * 2 == shards


def kernel(
    plan,
    q_ref,
    db_hbm,
    ids_ref,
    w_hbm,
    col_hbm,
    owner_ref,
    block_ref,
    out_ref,
    db,
    w_ref,
    col_ref,
    uq,
    part,
    rs_buf,
    z_send,
    z_buf,
    full,
    tiles,
    scores_ref,
    all1,
    all2,
    load_sem,
    rs_sems,
    z_sems,
    ag_sems,
    far_sems,
    mid_sems,
    core_sems,
):
    rows_dev, width = db.shape
    blocks_dev, tile_count, edge_count, block_rows = w_ref.shape
    slices, inner, outer = plan.slices, plan.inner, plan.outer
    region, shard = lax.axis_index("region"), lax.axis_index("shard")
    group_at, group = shard % inner, shard // inner
    slot = region * inner + group_at

    def member(index):
        return (index // inner, group * inner + index % inner)

    def across(index):
        return (region, index * inner + group_at)

    load = pltpu.make_async_copy(db_hbm, db, load_sem.at[0])
    load.start()
    tile_loads = [
        pltpu.make_async_copy(w_hbm, w_ref, load_sem.at[1]),
        pltpu.make_async_copy(col_hbm, col_ref, load_sem.at[2]),
    ]
    for tile_load in tile_loads:
        tile_load.start()
    barrier = pltpu.get_barrier_semaphore()
    for d in range(1, slices):
        pl.semaphore_signal(
            barrier, inc=1, device_id=member(flip(slot, d)), device_id_type=pl.DeviceIdType.MESH
        )
    for d in range(1, outer):
        pl.semaphore_signal(
            barrier, inc=1, device_id=across(flip(group, d)), device_id_type=pl.DeviceIdType.MESH
        )

    def send(src, dst, sems, at, device):
        copy = pltpu.make_async_remote_copy(
            src_ref=src,
            dst_ref=dst,
            send_sem=sems.at[(0,) + at],
            recv_sem=sems.at[(1,) + at],
            device_id=device,
            device_id_type=pl.DeviceIdType.MESH,
        )
        copy.start()
        return copy

    row_of = lax.broadcasted_iota(jnp.int32, (block_rows, block_rows), 0).astype(F32).astype(BF16)

    def build(t, carry):
        b, j = t // tile_count, t % tile_count
        columns = col_ref[b, j].astype(F32).astype(BF16)
        weights = w_ref[b, j]
        acc = None
        for e in range(edge_count):
            hit = row_of == columns[e : e + 1, :]
            term = jnp.where(hit, weights[e : e + 1, :], jnp.zeros((), BF16))
            acc = term if acc is None else acc + term
        tiles[t] = acc
        return carry

    total_tiles = blocks_dev * tile_count
    cuts = [total_tiles * part_of // 26 for part_of in CUTS]

    q = q_ref[...].astype(F32)
    unit = (q / jnp.sqrt(jnp.sum(q * q, axis=1, keepdims=True) + EPS)).astype(BF16)
    for p in range(slices):
        uq[p] = unit[:, p * LANES : (p + 1) * LANES].astype(F32)
    ids = ids_ref[...].T - (region * plan.shards + shard) * rows_dev
    row_ids = lax.broadcasted_iota(jnp.int32, (ids.shape[0], rows_dev), 1)
    counts = jnp.zeros((ids.shape[0], rows_dev), F32)
    for k in range(ids.shape[1]):
        counts = counts + jnp.where(ids[:, k : k + 1] == row_ids, 1.0, 0.0)
    load.wait()
    data = db[...]
    similar = lax.dot_general(unit, data, (((1,), (1,)), ((), ())), preferred_element_type=F32)
    positive = jnp.maximum(similar, 0.0)
    weights = (positive * positive * positive / math.sqrt(width)).astype(BF16)
    chosen = (counts * weights.astype(F32)).astype(BF16)
    local = jnp.dot(chosen, data, preferred_element_type=F32)
    for p in range(slices):
        part[p] = local[:, p * LANES : (p + 1) * LANES].astype(BF16)

    for tile_load in tile_loads:
        tile_load.wait()
    pl.semaphore_wait(barrier, slices - 1 + outer - 1)

    copies = []
    for d in range(1, slices):
        peer = flip(slot, d)
        copies.append(send(part.at[peer], rs_buf.at[d], rs_sems, (d,), member(peer)))
    lax.fori_loop(cuts[0], cuts[1], build, 0)
    total = part[slot].astype(F32)
    for d in range(1, slices):
        copies[d - 1].wait_recv()
        total = total + rs_buf[d].astype(F32)
    z_send[...] = total.astype(BF16)
    pending = copies

    copies = []
    for d in range(1, outer):
        copies.append(send(z_send, z_buf.at[d], z_sems, (d,), across(flip(group, d))))
    lax.fori_loop(cuts[1], cuts[2], build, 0)
    total = total + uq[slot]
    for d in range(1, outer):
        copies[d - 1].wait_recv()
        total = total + z_buf[d].astype(F32)
    full[slot] = total.astype(BF16)
    pending = pending + copies

    copies = []
    for d in range(1, slices):
        copies.append(
            send(full.at[slot], full.at[slot], ag_sems, (d,), member(flip(slot, d)))
        )
    lax.fori_loop(cuts[2], cuts[3], build, 0)
    for copy in copies:
        copy.wait_recv()
    pending = pending + copies

    expanded = jnp.concatenate([full[p] for p in range(slices)], axis=1)
    wide = expanded.astype(F32)
    scale = 1.0 / jnp.sqrt(jnp.sum(wide * wide, axis=1, keepdims=True) + EPS)
    products = lax.dot_general(
        expanded, data, (((1,), (1,)), ((), ())), preferred_element_type=F32
    )
    scores = jnp.maximum(products * scale, 0.0).astype(BF16)

    mid, far = plan.mid, plan.far
    far_at, mid_at, core_at = shard // (2 * mid), (shard // 2) % mid, shard % 2

    def share(buf, which, meanwhile=None):
        def place(f, m, c):
            return (f * mid + m) * 2 + c

        done = []

        def push(f, m, piece, sems, at, device):
            source = buf.at[place(f, m, core_at), piece]
            copy = send(source, source, sems, (which, piece) + at, (region, device))
            done.append(copy)
            return copy

        partner = place(far_at, mid_at, 1 - core_at)
        core_copies = []

        def to_mids(fd, piece):
            f = flip(far_at, fd)
            return [
                push(f, mid_at, piece, mid_sems, (md, fd), place(far_at, flip(mid_at, md), core_at))
                for md in range(1, mid)
            ]

        def to_core(md, fd, piece):
            f, m = flip(far_at, fd), flip(mid_at, md)
            core_copies.append(push(f, m, piece, core_sems, (md, fd), partner))

        order = [1] + list(range(far - 1, 1, -1)) if far > 1 else []
        steps = [(fd, piece) for fd in order for piece in range(blocks_dev)]
        far_copies = {
            (fd, piece): push(
                far_at, mid_at, piece, far_sems, (fd,), place(flip(far_at, fd), mid_at, core_at)
            )
            for fd, piece in steps
        }
        queue = []
        for piece in range(blocks_dev):
            queue.append((0, piece, to_mids(0, piece)))
        for piece in range(blocks_dev):
            to_core(0, 0, piece)
        if meanwhile is not None:
            meanwhile()

        def mids_arrive():
            fd, piece, copies = queue.pop(0)
            for md in range(1, mid):
                copies[md - 1].wait_recv()
                to_core(md, fd, piece)

        for at, (fd, piece) in enumerate(steps):
            far_copies[fd, piece].wait_recv()
            queue.append((fd, piece, to_mids(fd, piece)))
            to_core(0, fd, piece)
            if at >= LAG:
                mids_arrive()
        while queue:
            mids_arrive()
        for copy in core_copies:
            copy.wait_recv()
        return done

    def spread(buf):
        sums = []
        for b in range(blocks_dev):
            acc = None
            for j in range(tile_count):
                values = buf[owner_ref[b, j], block_ref[b, j]]
                term = jnp.dot(
                    values, tiles[b * tile_count + j], preferred_element_type=F32
                )
                acc = term if acc is None else acc + term
            sums.append(acc)
        return sums

    for b in range(blocks_dev):
        own = scores[:, b * block_rows : (b + 1) * block_rows]
        scores_ref[b] = own.astype(F32)
        all1[shard, b] = own
    pending = pending + share(all1, 0, lambda: lax.fori_loop(cuts[3], cuts[4], build, 0))
    sums = spread(all1)
    for b in range(blocks_dev):
        all2[shard, b] = (scores_ref[b] + BETA * sums[b]).astype(BF16)
    pending = pending + share(all2, 1)
    sums = spread(all2)
    for b in range(blocks_dev):
        out_ref[:, b * block_rows : (b + 1) * block_rows] = scores_ref[b] + BETA * sums[b]
    for copy in pending:
        copy.wait_send()


def per_device(
    plan, queries, database, neighbour_ids, tile_weights, tile_columns, tile_owner, tile_block
):
    query_count, width = queries.shape
    rows_dev = database.shape[0]
    blocks_dev, tile_count, edge_count, block_rows = tile_weights.shape
    vmem = pl.BlockSpec(memory_space=pltpu.VMEM)
    smem = pl.BlockSpec(memory_space=pltpu.SMEM)
    anywhere = pl.BlockSpec(memory_space=pl.ANY)
    dma = pltpu.SemaphoreType.DMA
    state = (plan.shards, blocks_dev, query_count, block_rows)
    piece = (query_count, LANES)
    return pl.pallas_call(
        functools.partial(kernel, plan),
        out_shape=jax.ShapeDtypeStruct((query_count, rows_dev), F32),
        in_specs=[vmem, anywhere, vmem, anywhere, anywhere, smem, smem],
        out_specs=vmem,
        scratch_shapes=[
            pltpu.VMEM((rows_dev, width), BF16),
            pltpu.VMEM(tile_weights.shape, BF16),
            pltpu.VMEM(tile_columns.shape, jnp.int32),
            pltpu.VMEM((plan.slices,) + piece, F32),
            pltpu.VMEM((plan.slices,) + piece, BF16),
            pltpu.VMEM((plan.slices,) + piece, BF16),
            pltpu.VMEM(piece, BF16),
            pltpu.VMEM((plan.outer,) + piece, BF16),
            pltpu.VMEM((plan.slices,) + piece, BF16),
            pltpu.VMEM((blocks_dev * tile_count, block_rows, block_rows), BF16),
            pltpu.VMEM((blocks_dev, query_count, block_rows), F32),
            pltpu.VMEM(state, BF16),
            pltpu.VMEM(state, BF16),
            dma((3,)),
            dma((2, plan.slices)),
            dma((2, plan.outer)),
            dma((2, plan.slices)),
            dma((2, 2, blocks_dev, plan.far)),
            dma((2, 2, blocks_dev, plan.mid, plan.far)),
            dma((2, 2, blocks_dev, plan.mid, plan.far)),
        ],
        compiler_params=pltpu.CompilerParams(collective_id=0, has_side_effects=True),
        name="expand_and_diffuse",
    )(queries, database, neighbour_ids.T, tile_weights, tile_columns, tile_owner, tile_block)


def solution(mesh):
    plan_of = functools.partial(Plan, mesh.shape["region"], mesh.shape["shard"])

    def body(queries, *rest):
        return per_device(plan_of(queries.shape[1]), queries, *rest)

    placed = (
        P(),
        P(("region", "shard"), None),
        P(),
        P(("region", "shard"), None, None, None),
        P(("region", "shard"), None, None, None),
        P(("region", "shard"), None),
        P(("region", "shard"), None),
    )
    return jax.shard_map(
        body,
        mesh=mesh,
        in_specs=placed,
        out_specs=P(None, ("region", "shard")),
        check_vma=False,
    )
```

```python
import functools
import math

import jax
import jax.numpy as jnp
from jax import lax
from jax.experimental import pallas as pl
from jax.experimental.pallas import tpu as pltpu
from jax.sharding import PartitionSpec as P

EPS = 1e-06
LAG = 1
BETA = 0.8
CUTS = (0, 0, 8, 16, 26)
LANES = 128
F32 = jnp.float32
BF16 = jnp.bfloat16


def flip(index, mask):
    bit = 1
    while bit <= mask:
        if mask & bit:
            index = index + bit - 2 * bit * ((index // bit) % 2)
        bit *= 2
    return index


class Plan:
    def __init__(self, regions, shards, width):
        self.regions, self.shards = regions, shards
        self.slices = width // LANES
        self.inner = self.slices // regions
        self.outer = shards // self.inner
        assert self.inner * regions * LANES == width and self.outer * self.inner == shards
        assert self.inner == 1 or self.inner % 2 == 0
        if self.inner > 2:
            self.mid = self.inner // 2
        else:
            self.mid = 1 << (((shards // 2).bit_length() - 1) // 2)
        self.far = shards // (2 * self.mid)
        assert self.far * self.mid * 2 == shards


def kernel(
    plan,
    q_ref,
    db_hbm,
    ids_ref,
    w_hbm,
    col_hbm,
    owner_hbm,
    block_hbm,
    out_ref,
    db,
    w_ref,
    col_ref,
    owner_ref,
    block_ref,
    uq,
    part,
    rs_buf,
    z_send,
    z_buf,
    full,
    tiles,
    scores_ref,
    all1,
    all2,
    load_sem,
    rs_sems,
    z_sems,
    ag_sems,
    far_sems,
    mid_sems,
    core_sems,
):
    rows_dev, width = db.shape
    blocks_dev, tile_count, edge_count, block_rows = w_ref.shape
    slices, inner, outer = plan.slices, plan.inner, plan.outer
    region, shard = lax.axis_index("region"), lax.axis_index("shard")
    group_at, group = shard % inner, shard // inner
    slot = region * inner + group_at

    def member(index):
        return (index // inner, group * inner + index % inner)

    def across(index):
        return (region, index * inner + group_at)

    load = pltpu.make_async_copy(db_hbm, db, load_sem.at[0])
    load.start()
    tile_loads = [
        pltpu.make_async_copy(w_hbm, w_ref, load_sem.at[1]),
        pltpu.make_async_copy(col_hbm, col_ref, load_sem.at[2]),
        pltpu.make_async_copy(owner_hbm, owner_ref, load_sem.at[3]),
        pltpu.make_async_copy(block_hbm, block_ref, load_sem.at[4]),
    ]
    for tile_load in tile_loads:
        tile_load.start()
    barrier = pltpu.get_barrier_semaphore()
    for d in range(1, slices):
        pl.semaphore_signal(
            barrier, inc=1, device_id=member(flip(slot, d)), device_id_type=pl.DeviceIdType.MESH
        )
    for d in range(1, outer):
        pl.semaphore_signal(
            barrier, inc=1, device_id=across(flip(group, d)), device_id_type=pl.DeviceIdType.MESH
        )

    def send(src, dst, sems, at, device):
        copy = pltpu.make_async_remote_copy(
            src_ref=src,
            dst_ref=dst,
            send_sem=sems.at[(0,) + at],
            recv_sem=sems.at[(1,) + at],
            device_id=device,
            device_id_type=pl.DeviceIdType.MESH,
        )
        copy.start()
        return copy

    row_of = lax.broadcasted_iota(jnp.int32, (block_rows, block_rows), 0).astype(F32).astype(BF16)

    def build(t, carry):
        b, j = t // tile_count, t % tile_count
        columns = col_ref[b, j].astype(F32).astype(BF16)
        weights = w_ref[b, j]
        acc = None
        for e in range(edge_count):
            hit = row_of == columns[e : e + 1, :]
            term = jnp.where(hit, weights[e : e + 1, :], jnp.zeros((), BF16))
            acc = term if acc is None else acc + term
        tiles[t] = acc
        return carry

    total_tiles = blocks_dev * tile_count
    cuts = [total_tiles * part_of // 26 for part_of in CUTS]

    q = q_ref[...].astype(F32)
    unit = (q / jnp.sqrt(jnp.sum(q * q, axis=1, keepdims=True) + EPS)).astype(BF16)
    for p in range(slices):
        uq[p] = unit[:, p * LANES : (p + 1) * LANES].astype(F32)
    ids = ids_ref[...].T - (region * plan.shards + shard) * rows_dev
    row_ids = lax.broadcasted_iota(jnp.int32, (ids.shape[0], rows_dev), 1)
    counts = jnp.zeros((ids.shape[0], rows_dev), F32)
    for k in range(ids.shape[1]):
        counts = counts + jnp.where(ids[:, k : k + 1] == row_ids, 1.0, 0.0)
    load.wait()
    data = db[...]
    similar = lax.dot_general(unit, data, (((1,), (1,)), ((), ())), preferred_element_type=F32)
    positive = jnp.maximum(similar, 0.0)
    weights = (positive * positive * positive / math.sqrt(width)).astype(BF16)
    chosen = (counts * weights.astype(F32)).astype(BF16)
    local = jnp.dot(chosen, data, preferred_element_type=F32)
    for p in range(slices):
        part[p] = local[:, p * LANES : (p + 1) * LANES].astype(BF16)

    pl.semaphore_wait(barrier, slices - 1 + outer - 1)

    copies = []
    for d in range(1, slices):
        peer = flip(slot, d)
        copies.append(send(part.at[peer], rs_buf.at[d], rs_sems, (d,), member(peer)))
    total = part[slot].astype(F32)
    for d in range(1, slices):
        copies[d - 1].wait_recv()
        total = total + rs_buf[d].astype(F32)
    z_send[...] = total.astype(BF16)
    pending = copies

    copies = []
    for d in range(1, outer):
        copies.append(send(z_send, z_buf.at[d], z_sems, (d,), across(flip(group, d))))
    for tile_load in tile_loads:
        tile_load.wait()
    lax.fori_loop(cuts[1], cuts[2], build, 0)
    total = total + uq[slot]
    for d in range(1, outer):
        copies[d - 1].wait_recv()
        total = total + z_buf[d].astype(F32)
    full[slot] = total.astype(BF16)
    pending = pending + copies

    copies = []
    for d in range(1, slices):
        copies.append(
            send(full.at[slot], full.at[slot], ag_sems, (d,), member(flip(slot, d)))
        )
    lax.fori_loop(cuts[2], cuts[3], build, 0)
    for copy in copies:
        copy.wait_recv()
    pending = pending + copies

    expanded = jnp.concatenate([full[p] for p in range(slices)], axis=1)
    wide = expanded.astype(F32)
    scale = 1.0 / jnp.sqrt(jnp.sum(wide * wide, axis=1, keepdims=True) + EPS)
    products = lax.dot_general(
        expanded, data, (((1,), (1,)), ((), ())), preferred_element_type=F32
    )
    scores = jnp.maximum(products * scale, 0.0).astype(BF16)

    mid, far = plan.mid, plan.far
    far_at, mid_at, core_at = shard // (2 * mid), (shard // 2) % mid, shard % 2

    def share(buf, which, meanwhile=None):
        def place(f, m, c):
            return (f * mid + m) * 2 + c

        done = []

        def push(f, m, piece, sems, at, device):
            source = buf.at[place(f, m, core_at)]
            copy = send(source, source, sems, (which, piece) + at, (region, device))
            done.append(copy)
            return copy

        partner = place(far_at, mid_at, 1 - core_at)
        core_copies = []

        def to_mids(fd, piece):
            f = flip(far_at, fd)
            return [
                push(f, mid_at, piece, mid_sems, (md, fd), place(far_at, flip(mid_at, md), core_at))
                for md in range(1, mid)
            ]

        def to_core(md, fd, piece):
            f, m = flip(far_at, fd), flip(mid_at, md)
            core_copies.append(push(f, m, piece, core_sems, (md, fd), partner))

        order = list(range(1, far))
        steps = [(fd, piece) for fd in order for piece in range(1)]
        far_copies = {
            (fd, piece): push(
                far_at, mid_at, piece, far_sems, (fd,), place(flip(far_at, fd), mid_at, core_at)
            )
            for fd, piece in steps
        }
        queue = []
        for piece in range(1):
            queue.append((0, piece, to_mids(0, piece)))
        for piece in range(1):
            to_core(0, 0, piece)
        if meanwhile is not None:
            meanwhile()

        def mids_arrive():
            fd, piece, copies = queue.pop(0)
            for md in range(1, mid):
                copies[md - 1].wait_recv()
                to_core(md, fd, piece)

        for at, (fd, piece) in enumerate(steps):
            far_copies[fd, piece].wait_recv()
            queue.append((fd, piece, to_mids(fd, piece)))
            to_core(0, fd, piece)
            if at >= LAG:
                mids_arrive()
        while queue:
            mids_arrive()
        for copy in core_copies:
            copy.wait_recv()
        return done

    def spread(buf):
        sums = []
        for b in range(blocks_dev):
            acc = None
            for j in range(tile_count):
                values = buf[owner_ref[b, j], block_ref[b, j]]
                term = jnp.dot(
                    values, tiles[b * tile_count + j], preferred_element_type=F32
                )
                acc = term if acc is None else acc + term
            sums.append(acc)
        return sums

    for b in range(blocks_dev):
        own = scores[:, b * block_rows : (b + 1) * block_rows]
        scores_ref[b] = own.astype(F32)
        all1[shard, b] = own
    pending = pending + share(all1, 0, lambda: lax.fori_loop(cuts[3], cuts[4], build, 0))
    sums = spread(all1)
    for b in range(blocks_dev):
        all2[shard, b] = (scores_ref[b] + BETA * sums[b]).astype(BF16)
    pending = pending + share(all2, 1)
    sums = spread(all2)
    for b in range(blocks_dev):
        out_ref[:, b * block_rows : (b + 1) * block_rows] = scores_ref[b] + BETA * sums[b]
    for copy in pending:
        copy.wait_send()


def per_device(
    plan, queries, database, neighbour_ids, tile_weights, tile_columns, tile_owner, tile_block
):
    query_count, width = queries.shape
    rows_dev = database.shape[0]
    blocks_dev, tile_count, edge_count, block_rows = tile_weights.shape
    vmem = pl.BlockSpec(memory_space=pltpu.VMEM)
    anywhere = pl.BlockSpec(memory_space=pl.ANY)
    dma = pltpu.SemaphoreType.DMA
    state = (plan.shards, blocks_dev, query_count, block_rows)
    piece = (query_count, LANES)
    return pl.pallas_call(
        functools.partial(kernel, plan),
        out_shape=jax.ShapeDtypeStruct((query_count, rows_dev), F32),
        in_specs=[vmem, anywhere, vmem, anywhere, anywhere, anywhere, anywhere],
        out_specs=vmem,
        scratch_shapes=[
            pltpu.VMEM((rows_dev, width), BF16),
            pltpu.VMEM(tile_weights.shape, BF16),
            pltpu.VMEM(tile_columns.shape, jnp.int32),
            pltpu.SMEM(tile_owner.shape, jnp.int32),
            pltpu.SMEM(tile_block.shape, jnp.int32),
            pltpu.VMEM((plan.slices,) + piece, F32),
            pltpu.VMEM((plan.slices,) + piece, BF16),
            pltpu.VMEM((plan.slices,) + piece, BF16),
            pltpu.VMEM(piece, BF16),
            pltpu.VMEM((plan.outer,) + piece, BF16),
            pltpu.VMEM((plan.slices,) + piece, BF16),
            pltpu.VMEM((blocks_dev * tile_count, block_rows, block_rows), BF16),
            pltpu.VMEM((blocks_dev, query_count, block_rows), F32),
            pltpu.VMEM(state, BF16),
            pltpu.VMEM(state, BF16),
            dma((5,)),
            dma((2, plan.slices)),
            dma((2, plan.outer)),
            dma((2, plan.slices)),
            dma((2, 2, 1, plan.far)),
            dma((2, 2, 1, plan.mid, plan.far)),
            dma((2, 2, 1, plan.mid, plan.far)),
        ],
        compiler_params=pltpu.CompilerParams(collective_id=0, has_side_effects=True),
        name="expand_and_diffuse",
    )(queries, database, neighbour_ids.T, tile_weights, tile_columns, tile_owner, tile_block)


def solution(mesh):
    plan_of = functools.partial(Plan, mesh.shape["region"], mesh.shape["shard"])

    def body(queries, *rest):
        return per_device(plan_of(queries.shape[1]), queries, *rest)

    placed = (
        P(),
        P(("region", "shard"), None),
        P(),
        P(("region", "shard"), None, None, None),
        P(("region", "shard"), None, None, None),
        P(("region", "shard"), None),
        P(("region", "shard"), None),
    )
    return jax.shard_map(
        body,
        mesh=mesh,
        in_specs=placed,
        out_specs=P(None, ("region", "shard")),
        check_vma=False,
    )
```
